32 devices in a mesh: dp: 2 (over x), tensor: 4 (over z), fsdp: 4 (over y, core).
Axes of the slice: x: 2, y: 2, z: 4, core: 2. Of those that a mesh axis runs over, the one named last changes fastest.
Arguments:
- train_acts: bfloat16 [2048, 4096], P(('dp', 'fsdp'), 'tensor'), may hold values from -6 to 6
- val_acts: bfloat16 [2048, 4096], P(('dp', 'fsdp'), 'tensor'), may hold values from -6 to 6
- train_cot: bfloat16 [2048, 4096], P(('dp', 'fsdp'), 'tensor'), may hold values from -6 to 6
- val_cot: bfloat16 [2048, 4096], P(('dp', 'fsdp'), 'tensor'), may hold values from -6 to 6
- train_lengths: int32 [32], P(('dp', 'fsdp')), may hold values from 16 to 64
- val_lengths: int32 [32], P(('dp', 'fsdp')), may hold values from 16 to 64
- gate_weight: bfloat16 [4096, 11008], P(('dp', 'fsdp'), 'tensor'), may hold values from -0.09375 to 0.09375
- up_weight: bfloat16 [4096, 11008], P(('dp', 'fsdp'), 'tensor'), may hold values from -0.09375 to 0.09375
- in_basis: bfloat16 [11008, 64], P('tensor'), may hold values from -0.0546875 to 0.0546875
- out_basis: bfloat16 [4096, 128], P('tensor'), may hold values from -0.09375 to 0.09375
Outputs:
- scores: float32 [32, 32], P(('dp', 'fsdp'))
The draws below stay inside these ranges and needn't reach their ends.
Inputs may be any that keep to these rules, and one draw needn't show every extreme that they name: `train_lengths`: an example's first length slots hold its tokens, the rest are padding. `val_lengths`: as for the training examples.
All inputs are finite; a program needn't handle non-finite values.
Results may differ from the reference program's by a relative error of at most 0.004.
Values may be sent and summed in bfloat16 or wider, within the bound.
No kernel may reach another device: no remote copies, remote signals or barrier semaphores. Data moves between devices by JAX's collectives and lax.ppermute only.
A program may use at most 128 MiB of HBM per device.

```python
import jax
import jax.numpy as jnp
from jax import lax

D = 4096
FF = 11008
K_IN = 64
K_OUT = 128
SEQ = 64
TRAIN = 32
VAL = 32


def touch_ends(entries, key, low, largest):
    longest = entries.shape.index(max(entries.shape))
    spots = []
    for shift in (0, 1):
        where = [jax.random.randint(jax.random.fold_in(key, axis), (), 0, length) for axis, length in enumerate(entries.shape)]
        where[longest] = (where[longest] + shift) % entries.shape[longest]
        spots.append(tuple(where))
    return entries.at[spots[0]].set(low).at[spots[1]].set(largest)


def shard_levels(key, dims, split, low, largest):
    loudness, own = 1.0, jax.random.fold_in(key, 6)
    for dim, shards_of in split:
        heights = jnp.exp(jax.random.uniform(jax.random.fold_in(own, dim), (shards_of,), jnp.float32, low / len(split), largest / len(split)))
        loudness = loudness * jnp.repeat(heights, dims[dim] // shards_of).reshape([-1 if axis == dim else 1 for axis in range(len(dims))])
    return loudness


def scatter_about(rng, dims, width, limit, cuts=(), kind=jnp.bfloat16):
    level = shard_levels(rng, dims, cuts, -0.22, 0.18) if cuts else 1.0
    values = jax.random.normal(rng, dims, jnp.float32) * width * level
    return jnp.minimum(jnp.maximum(values, -limit), limit).astype(kind)


def setup_inputs(seed: int = 0) -> dict:
    splits = jax.random.split(jax.random.key(seed), 11)
    train_acts = scatter_about(splits[0], (TRAIN * SEQ, D), 1.0, 6.0, ((0, 8), (1, 4)))
    val_acts = scatter_about(splits[1], (VAL * SEQ, D), 1.0, 6.0, ((0, 8), (1, 4)))
    train_cot = scatter_about(splits[2], (TRAIN * SEQ, D), 1.0, 6.0, ((0, 8), (1, 4)))
    val_cot = scatter_about(splits[3], (VAL * SEQ, D), 1.0, 6.0, ((0, 8), (1, 4)))
    train_lengths = touch_ends(jax.random.randint(splits[4], (TRAIN,), SEQ // 4, SEQ + 1), jax.random.fold_in(splits[4], 1), SEQ // 4, SEQ).astype(jnp.int32)
    val_lengths = touch_ends(jax.random.randint(splits[5], (VAL,), SEQ // 4, SEQ + 1), jax.random.fold_in(splits[5], 1), SEQ // 4, SEQ).astype(jnp.int32)
    gate_weight = scatter_about(splits[6], (D, FF), D ** -0.5, 0.09375, ((0, 8), (1, 4)))
    up_weight = scatter_about(splits[7], (D, FF), D ** -0.5, 0.09375, ((0, 8), (1, 4)))
    in_basis = scatter_about(splits[8], (FF, K_IN), FF ** -0.5, 0.0546875, ((0, 4),))
    out_basis = scatter_about(splits[9], (D, K_OUT), D ** -0.5, 0.09375, ((0, 4),))
    return dict(train_acts=train_acts, val_acts=val_acts, train_cot=train_cot, val_cot=val_cot, train_lengths=train_lengths, val_lengths=val_lengths, gate_weight=gate_weight, up_weight=up_weight, in_basis=in_basis, out_basis=out_basis)


def sketch_rows(activations, cotangents, lengths, gate_weight, up_weight, in_basis, out_basis):
    gate_sum = jnp.dot(activations, gate_weight, preferred_element_type=jnp.float32)
    up_sum = jnp.dot(activations, up_weight, preferred_element_type=jnp.float32)
    hidden = (jax.nn.silu(gate_sum) * up_sum).astype(jnp.bfloat16)
    in_proj = jnp.dot(hidden, in_basis, preferred_element_type=jnp.float32)
    out_proj = jnp.dot(cotangents, out_basis, preferred_element_type=jnp.float32)
    valid = (jnp.arange(SEQ, dtype=jnp.int32)[None, :] < lengths[:, None]).astype(jnp.float32)
    in_three = in_proj.reshape(-1, SEQ, K_IN) * valid[:, :, None]
    out_three = out_proj.reshape(-1, SEQ, K_OUT)
    sketch = jnp.einsum('esj,esk->ejk', in_three, out_three, precision=lax.Precision.HIGHEST)
    sketch = sketch.reshape(sketch.shape[0], K_IN * K_OUT)
    return sketch * lax.rsqrt(lax.optimization_barrier(jnp.sum(sketch * sketch, axis=1, keepdims=True)) + 1e-06)

def reference(train_acts, val_acts, train_cot, val_cot, train_lengths, val_lengths, gate_weight, up_weight, in_basis, out_basis):
    train_unit = sketch_rows(train_acts, train_cot, train_lengths, gate_weight, up_weight, in_basis, out_basis)
    val_unit = sketch_rows(val_acts, val_cot, val_lengths, gate_weight, up_weight, in_basis, out_basis)
    product = jnp.dot(train_unit, val_unit.T, precision=lax.Precision.HIGHEST, preferred_element_type=jnp.float32)
    return product * jnp.sqrt(jnp.float32(K_IN * K_OUT))
```

```python
import functools

import jax
import jax.numpy as jnp
from jax import lax
from jax.experimental import pallas as pl
from jax.experimental.pallas import tpu as pltpu
from jax.sharding import PartitionSpec as P

SEQ = 64
CHUNK = 256
HIGH = lax.Precision.HIGHEST
F32 = jnp.float32


def nt_dot(a, b, **options):
    return lax.dot_general(a, b, (((1,), (1,)), ((), ())), preferred_element_type=F32, **options)


def hidden_kernel(steps, piece, part, a_ref, lo_ref, hi_ref, basis_ref, out_ref, total):
    k = pl.program_id(0)
    acts = a_ref[0]

    @pl.when(k == 0)
    def _():
        total[...] = nt_dot(lo_ref[0], acts)

    @pl.when((k > 0) & (k < steps // 2))
    def _():
        total[...] += nt_dot(lo_ref[0], acts)

    @pl.when(k >= steps // 2)
    def _():
        total[...] += nt_dot(hi_ref[0], acts)

    @pl.when(k == steps - 1)
    def _():
        columns = total.shape[0] // 2
        gate = total[:columns]
        hidden = (gate / (1.0 + jnp.exp(-gate)) * total[columns:]).astype(jnp.bfloat16)
        out_ref[...] = jnp.dot(basis_ref[...], hidden, preferred_element_type=F32)


def hidden_chunk(piece, part, acts, low, high, basis):
    steps = 2 * low.shape[0]
    half = low.shape[0]
    rows, depth = low.shape[1:]
    tokens = acts.shape[1]
    grid_spec = pltpu.PrefetchScalarGridSpec(
        num_scalar_prefetch=2,
        grid=(steps,),
        in_specs=[
            pl.BlockSpec((1, tokens, depth), lambda k, piece, part: (piece[k], 0, part[k])),
            pl.BlockSpec((1, rows, depth), lambda k, *_: (jnp.minimum(k, half - 1), 0, 0)),
            pl.BlockSpec((1, rows, depth), lambda k, *_: (jnp.maximum(k - half, 0), 0, 0)),
            pl.BlockSpec(basis.shape, lambda k, *_: (0, 0)),
        ],
        out_specs=pl.BlockSpec((basis.shape[0], tokens), lambda k, *_: (0, 0)),
        scratch_shapes=[pltpu.VMEM((rows, tokens), F32)],
    )
    flops = 2 * tokens * rows * depth * steps
    return pl.pallas_call(
        functools.partial(hidden_kernel, steps),
        grid_spec=grid_spec,
        out_shape=jax.ShapeDtypeStruct((basis.shape[0], tokens), F32),
        compiler_params=pltpu.CompilerParams(
            dimension_semantics=("arbitrary",), vmem_limit_bytes=40 * 1024 * 1024
        ),
        cost_estimate=pl.CostEstimate(
            flops=flops,
            bytes_accessed=2 * steps * depth * (tokens + rows),
            transcendentals=tokens * rows // 2,
        ),
        name="hidden_chunk",
    )(piece, part, acts, low, high, basis)


def xor_pairs(size, bit):
    return [(i, i ^ bit) for i in range(size)]


def relay(block, size, here):
    up_pairs = [(i, i + 1) for i in range(size - 1)]
    down_pairs = [(i + 1, i) for i in range(size - 1)]
    from_below, from_above = [block], [block]
    for _ in range(size - 1):
        from_below.append(lax.ppermute(from_below[-1], "tensor", up_pairs))
        from_above.append(lax.ppermute(from_above[-1], "tensor", down_pairs))
    blocks = [block]
    for r in range(1, size):
        blocks.append(jnp.where(here + r < size, from_above[r], from_below[size - r]))
    return jnp.stack(blocks)


def all_sum(value, axis, size):
    bit = 1
    while bit < size:
        value = value + lax.ppermute(value, axis, xor_pairs(size, bit))
        bit *= 2
    return value


def on_device(
    sizes,
    train_acts,
    val_acts,
    train_cot,
    val_cot,
    train_lengths,
    val_lengths,
    gate_weight,
    up_weight,
    in_basis,
    out_basis,
):
    n_d, n_t, n_f = sizes
    d, t, f = lax.axis_index("dp"), lax.axis_index("tensor"), lax.axis_index("fsdp")
    depth, columns_all = gate_weight.shape
    columns = columns_all // n_d
    per_block = n_d * n_f // n_t
    k_in, k_out = in_basis.shape[1], out_basis.shape[1]
    shift = lambda s: [(i, (i + s) % n_d) for i in range(n_d)]

    own = jnp.concatenate([train_acts, val_acts], axis=0)
    tokens = own.shape[0]
    others = [lax.ppermute(own, "dp", shift(s)) for s in range(1, n_d)]

    gate_t, up_t, basis_t = gate_weight.T, up_weight.T, in_basis.T
    chunks, start = [], 0
    while start < columns:
        chunks.append((start, min(CHUNK, columns - start)))
        start += CHUNK

    def pack(owner, chunk):
        first = owner * columns + chunk[0]
        return jnp.concatenate(
            [lax.dynamic_slice_in_dim(w, first, chunk[1], 0) for w in (gate_t, up_t)], axis=0
        )

    blocks = []
    for chunk in chunks:
        mine = [pack(d, chunk)]
        for s in range(1, n_d):
            mine.append(lax.ppermute(pack((d + s) % n_d, chunk), "dp", shift(s)))
        blocks.append(mine)
    order = [((d - s) % n_d, f) for s in range(n_d)]
    bit = n_f // 2
    while bit > 1:
        pairs = xor_pairs(n_f, bit)
        for mine in blocks:
            mine.extend([lax.ppermute(block, "fsdp", pairs) for block in list(mine)])
        order = order + [(dd, ff ^ bit) for dd, ff in order]
        bit //= 2
    order = order + [(dd, ff ^ 1) for dd, ff in order]
    rows_of = jnp.stack([dd * n_f + ff for dd, ff in order]).astype(jnp.int32)
    piece = (rows_of // per_block - t) % n_t
    part = rows_of % per_block

    groups = [relay(own, n_t, t)]
    if others:
        groups.append(relay(jnp.concatenate(others, axis=0), n_t, t))

    sums = [0.0] * len(groups)
    for chunk, mine in zip(chunks, blocks):
        low = jnp.stack(mine)
        high = lax.ppermute(low, "fsdp", xor_pairs(n_f, 1))
        basis = lax.dynamic_slice_in_dim(basis_t, d * columns + chunk[0], chunk[1], 1)
        for g, acts in enumerate(groups):
            sums[g] = sums[g] + hidden_chunk(piece, part, acts, low, high, basis)

    in_t = sums[0]
    for s in range(1, n_d):
        back = sums[1][:, (s - 1) * tokens : s * tokens]
        in_t = in_t + lax.ppermute(back, "dp", shift(n_d - s))
    bit = n_t // 2
    while bit >= 1:
        half = in_t.shape[0] // 2
        upper = (t // bit) % 2
        keep = lax.dynamic_slice_in_dim(in_t, upper * half, half, 0)
        give = lax.dynamic_slice_in_dim(in_t, (1 - upper) * half, half, 0)
        in_t = keep + lax.ppermute(give, "tensor", xor_pairs(n_t, bit))
        bit //= 2
    share = in_t.shape[0]

    cotangents = jnp.concatenate([train_cot, val_cot], axis=0)
    out_part = jnp.dot(cotangents, out_basis, preferred_element_type=F32)
    out_proj = all_sum(out_part, "tensor", n_t)

    lengths = jnp.concatenate([train_lengths, val_lengths], axis=0)
    examples = lengths.shape[0]
    valid = (jnp.arange(SEQ, dtype=jnp.int32)[None, :] < lengths[:, None]).astype(F32)
    in_three = in_t.reshape(share, examples, SEQ) * valid[None]
    out_three = out_proj.reshape(examples, SEQ, k_out)
    sketch = jnp.einsum("jes,esk->ejk", in_three, out_three, precision=HIGH)

    train_count = train_lengths.shape[0]
    train_share = sketch[:train_count].reshape(train_count, share * k_out)
    val_share = sketch[train_count:].reshape(examples - train_count, share * k_out)
    val_all = lax.all_gather(val_share, ("dp", "fsdp"), axis=0, tiled=True)
    products = nt_dot(train_share, val_all, precision=HIGH)
    train_square = jnp.sum(train_share * train_share, axis=1, keepdims=True)
    val_square = jnp.sum(val_all * val_all, axis=1)[None]
    val_count = val_all.shape[0]
    packed = jnp.concatenate(
        [
            jnp.concatenate([products, train_square], axis=1),
            jnp.concatenate([val_square, jnp.zeros((1, 1), F32)], axis=1),
        ],
        axis=0,
    )
    packed = all_sum(packed, "tensor", n_t)
    train_scale = lax.rsqrt(packed[:train_count, val_count:] + 1e-06)
    val_scale = lax.rsqrt(packed[train_count:, :val_count] + 1e-06)
    return packed[:train_count, :val_count] * train_scale * val_scale * jnp.sqrt(F32(k_in * k_out))


def solution(mesh):
    sizes = tuple(mesh.shape[name] for name in ("dp", "tensor", "fsdp"))
    rows, cols = P(("dp", "fsdp"), "tensor"), P("tensor", None)
    counts = P(("dp", "fsdp"))
    placed = (rows, rows, rows, rows, counts, counts, rows, rows, cols, cols)
    return jax.shard_map(
        functools.partial(on_device, sizes),
        mesh=mesh,
        in_specs=placed,
        out_specs=P(("dp", "fsdp"), None),
        check_vma=False,
    )
```
